512 devices in a mesh: row: 32 (over x, y, core), col: 16 (over z).
Axes of the slice: x: 4, y: 4, z: 16, core: 2. Of those that a mesh axis runs over, the one named last changes fastest.
Arguments:
- features: bfloat16 [3, 32, 128, 512], P(None, 'row', 'col'), may hold values from -6 to 6
Outputs:
- panels: float32 [3, 32, 128, 256], P(None, 'row')
- trailing: float32 [3, 32, 128, 6, 16, 128], P(None, 'row', None, None, 'col')
The draws below stay inside these ranges and needn't reach their ends.
All inputs are finite; a program needn't handle non-finite values.
Results may differ from the reference program's by a relative error of at most 0.0003.
Values may be sent and summed in bfloat16 or wider, within the bound.
A program may use at most 64 MiB of HBM per device.

```python
import math
import jax
import jax.numpy as jnp
from jax import lax

N = 12288
F = 512
TILE = 128
PANEL = 256
PANELS = 1
LAYERS = 2
RT = 3
CT = 6
N_ROW = 32
N_COL = 16


def steps_of(stream_key, dims, pieces, low, top_value):
    factor_of = 1.0
    for position, shards_of in pieces:
        steps = jax.random.uniform(jax.random.fold_in(jax.random.fold_in(stream_key, 6), position), (shards_of,), jnp.float32, low / len(pieces), top_value / len(pieces))
        factor_of = factor_of * jnp.repeat(jnp.exp(steps), dims[position] // shards_of).reshape((-1,) + (1,) * (len(dims) - 1 - position))
    return factor_of


def scatter_about(rng, extent, spread, reach, cuts=(), held_as=jnp.bfloat16):
    values = spread * jax.random.normal(rng, extent, jnp.float32)
    if cuts:
        values = values * steps_of(rng, extent, cuts, -0.22, 0.18)
    return jnp.clip(values, -reach, reach).astype(held_as)


def setup_inputs(seed: int = 0) -> dict:
    arg_keys = jax.random.split(jax.random.key(seed), 2)
    features = scatter_about(arg_keys[0], (RT, N_ROW, TILE, F), 1.0, 6.0, ((1, 32), (2, 16)))
    return {"features": features}


def kernel_rows(x_rows, q_rows, x_all, q_all, row_ids, col_ids):
    gram = jnp.dot(x_rows.astype(jnp.float32), x_all.T.astype(jnp.float32), preferred_element_type=jnp.float32) / F
    scale = jnp.sqrt(q_rows[:, None] * q_all[None, :])
    same = row_ids[:, None] == col_ids[None, :]
    rho = jnp.where(same, 1.0, gram / scale)
    theta = gram
    for layer in range(LAYERS):
        angle = jnp.arccos(rho)
        jfun = (jnp.sqrt(1.0 - rho * rho) + (math.pi - angle) * rho) / math.pi
        theta = theta * (math.pi - angle) / math.pi + scale * jfun
        rho = jfun
    return theta + jnp.where(same, 1.0, 0.0)

def reference(features):
    x_all = features.reshape(N, F)
    q_all = lax.optimization_barrier(jnp.sum(x_all.astype(jnp.float32) ** 2, axis=1)) / F + 1e-06
    col_ids = jnp.arange(N, dtype=jnp.int32)
    block = 1024 if N % 1024 == 0 else N
    starts = jnp.arange(N // block, dtype=jnp.int32) * block

    def one_block(start):
        xs = lax.dynamic_slice_in_dim(x_all, start, block, 0)
        qs = lax.dynamic_slice_in_dim(q_all, start, block, 0)
        ids = start + jnp.arange(block, dtype=jnp.int32)
        return kernel_rows(xs, qs, x_all, q_all, ids, col_ids)
    kmat = lax.map(one_block, starts).reshape(N, N)
    outs = []
    for panel in range(PANELS):
        lo = panel * PANEL
        chol = jnp.linalg.cholesky(kmat[lo:lo + PANEL, lo:lo + PANEL])
        lower = lax.linalg.triangular_solve(chol, kmat[:, lo:lo + PANEL], left_side=False, lower=True, transpose_a=True)
        lower = jnp.where(col_ids[:, None] < lo, 0.0, lower)
        kmat = kmat - jnp.dot(lower, lower.T, precision=lax.Precision.HIGHEST)
        outs.append(lower)
    panels = jnp.concatenate(outs, axis=1).reshape(RT, N_ROW, TILE, PANELS * PANEL)
    return (panels, kmat.reshape(RT, N_ROW, TILE, CT, N_COL, TILE))
```

```python
import functools, math
import jax, jax.numpy as jnp
from jax import lax
from jax.experimental import pallas as pl
from jax.experimental.pallas import tpu as pltpu
from jax.sharding import PartitionSpec as P
MESH = pl.DeviceIdType.MESH
NZ = 16

def comm_kernel(H, x_ref, R, C, Q, lsem, zrecv, zsend, crecv, csend, qrecv, qsend, lc_sem):
    r = lax.axis_index("row")
    z = lax.axis_index("col")
    core = r % 2
    y = (r // 2) % 4
    x = r // 8

    def rid(xx, yy, cc):
        return (((xx + 4) % 4) * 4 + ((yy + 4) % 4)) * 2 + cc

    own = pltpu.make_async_copy(x_ref.at[:, 0], R.at[z], lsem)
    own.start()
    bar = pltpu.get_barrier_semaphore()
    peers = []
    zs = [j for j in range(1, H + 1)] + [16 - j for j in range(1, H + 1)]
    for j in sorted(set(zs)):
        peers.append((r, (z + j) % 16))
    for j in (1, 2, 3):
        peers.append((rid(x, y + j, core), z))
        peers.append((rid(x + j, y, core), z))
    peers.append((rid(x, y, 1 - core), z))
    for p in peers:
        pl.semaphore_signal(bar, inc=1, device_id=p, device_id_type=MESH)
    pl.semaphore_wait(bar, len(peers))
    own.wait()

    def zcopy(o, d, j):
        return pltpu.make_async_remote_copy(
            src_ref=R.at[o], dst_ref=R.at[o], send_sem=zsend.at[(0 if d > 0 else H) + j - 1],
            recv_sem=zrecv.at[o], device_id=(r, (z + d * j + 16) % 16), device_id_type=MESH)

    xs0, ys, cs = z // 8, (z // 2) % 4, z % 2
    streams = []
    for t in range(2):
        streams.append((qrecv, qsend, t, Q, 0, 0, t))
    for b in range(2):
        streams.append((crecv, csend, b, C, xs0 + 2 * b, ys, cs))

    def targets():
        ts = [(rid(x, y + j, core), z) for j in (1, 2, 3)]
        ts += [(rid(x + j, y, core), z) for j in (1, 2, 3)]
        ts += [(rid(x, y, 1 - core), z)]
        return ts

    def src_of(S, o):
        rs, ss, i, buf, rx, ry, rc = S
        return R.at[o, 0] if buf is Q else R.at[o]

    def pcopy(S, o, k, src):
        rs, ss, i, buf, rx, ry, rc = S
        return pltpu.make_async_remote_copy(
            src_ref=src, dst_ref=buf.at[i, o], send_sem=ss.at[i, k], recv_sem=rs.at[i, o],
            device_id=targets()[k], device_id_type=MESH)

    def roles(S):
        rs, ss, i, buf, rx, ry, rc = S
        oncore = core == rc
        is_src = oncore & (x == rx) & (y == ry)
        is_y = oncore & (x == rx) & (y != ry)
        is_x = oncore & (x != rx)
        is_s = core != rc
        return is_src, is_y, is_x, is_s

    def local_copy(S, o):
        rs, ss, i, buf, rx, ry, rc = S
        return pltpu.make_async_copy(src_of(S, o), buf.at[i, o], rs.at[i, o])

    def at_source(o):
        for S in streams:
            @pl.when(roles(S)[0])
            def _():
                for k in range(7):
                    pcopy(S, o, k, src_of(S, o)).start()
                local_copy(S, o).start()

    def wait_block(S, o):
        rs, ss, i, buf, rx, ry, rc = S
        pltpu.make_async_copy(buf.at[i, o], buf.at[i, o], rs.at[i, o]).wait()

    def relay(which, o):
        for S in streams:
            role = roles(S)[which]
            buf, i = S[3], S[2]
            @pl.when(role)
            def _():
                wait_block(S, o)
                ks = {1: (3, 4, 5, 6), 2: (6,), 3: ()}[which]
                for k in ks:
                    pcopy(S, o, k, buf.at[i, o]).start()

    for j in range(1, H + 1):
        zcopy(z, 1, j).start()
        if j <= 7:
            zcopy(z, -1, j).start()
    at_source(z)

    def seq(i):
        d = (i + 1) // 2
        return lax.rem(jnp.where(i % 2 == 1, z - d, z + d) + 16, 16)

    def step(i, _):
        @pl.when((i >= 1) & (i < 16))
        def _():
            o = seq(i)
            d = (i + 1) // 2
            pltpu.make_async_copy(R.at[o], R.at[o], zrecv.at[o]).wait()
            fwd = (d % H == 0)
            @pl.when(fwd & (i % 2 == 1))
            def _():
                for j in range(1, H + 1):
                    @pl.when(d + j <= 8)
                    def _():
                        zcopy(o, 1, j).start()
            @pl.when(fwd & (i % 2 == 0))
            def _():
                for j in range(1, min(H, 7) + 1):
                    @pl.when(d + j <= 7)
                    def _():
                        zcopy(o, -1, j).start()
            at_source(o)
        for which, lag in ((1, 2), (2, 4), (3, 5)):
            @pl.when((i >= lag) & (i < 16 + lag))
            def _():
                relay(which, seq(i - lag))
        return 0

    lax.fori_loop(0, 21, step, 0)

    for S in streams:
        @pl.when(roles(S)[0])
        def _():
            def w(o, _):
                wait_block(S, o)
                return 0
            lax.fori_loop(0, 16, w, 0)
    for d, lim in ((1, 8), (-1, 7)):
        for j in range(1, H + 1):
            n = (1 if j <= lim else 0) + sum(1 for dd in range(H, lim, H) if dd + j <= lim)
            if n:
                v = R.at[pl.ds(0, n)]
                pltpu.make_async_copy(v, v, zsend.at[(0 if d > 0 else H) + j - 1]).wait()
    for S in streams:
        rs, ss, i, buf, rx, ry, rc = S
        is_src, is_y, is_x, is_s = roles(S)
        for k in range(7):
            cond = is_src if k < 3 else ((is_src | is_y) if k < 6 else (core == rc))
            @pl.when(cond)
            def _():
                pltpu.make_async_copy(buf.at[i], buf.at[i], ss.at[i, k]).wait()


def gather(features, H=1):
    vm = pl.BlockSpec(memory_space=pltpu.VMEM)
    return pl.pallas_call(
        functools.partial(comm_kernel, H),
        out_shape=(jax.ShapeDtypeStruct((16, 3, 8, 512), jnp.bfloat16),
                   jax.ShapeDtypeStruct((2, 16, 3, 8, 512), jnp.bfloat16),
                   jax.ShapeDtypeStruct((2, 16, 8, 512), jnp.bfloat16)),
        in_specs=[pl.BlockSpec(memory_space=pl.ANY)],
        out_specs=(vm, vm, vm),
        scratch_shapes=[pltpu.SemaphoreType.DMA, pltpu.SemaphoreType.DMA((16,)), pltpu.SemaphoreType.DMA((2 * H,)),
                        pltpu.SemaphoreType.DMA((2, 16)), pltpu.SemaphoreType.DMA((2, 7)),
                        pltpu.SemaphoreType.DMA((2, 16)), pltpu.SemaphoreType.DMA((2, 7)),
                        pltpu.SemaphoreType.DMA],
        compiler_params=pltpu.CompilerParams(collective_id=0, has_side_effects=True),
        name="gather_features",
    )(features)


F = 512
F32 = jnp.float32
BF = jnp.bfloat16
IPI = 1.0 / math.pi
POLY = (1.5707963050, -0.2145988016, 0.0889789874, -0.0501743046,
        0.0308918810, -0.0170881256, 0.0066700901, -0.0012624911)
NT = (((1,), (1,)), ((), ()))
NN = (((1,), (0,)), ((), ()))
TN = (((0,), (0,)), ((), ()))


def dot(a, b, dims):
    return lax.dot_general(a, b, dims, preferred_element_type=F32)


def split(a):
    hi = a.astype(BF)
    return hi, (a - hi.astype(F32)).astype(BF)


def dot3(a, b, dims):
    return dot(a[0], b[0], dims) + (dot(a[0], b[1], dims) + dot(a[1], b[0], dims))


def half_angle(ax):
    y = jnp.maximum(1.0 - ax, 1e-30)
    s = y * lax.rsqrt(y)
    z = 1.0 + ax
    root = (s * IPI) * (z * lax.rsqrt(z))
    p = POLY[7] * IPI
    for c in POLY[6::-1]:
        p = p * ax + c * IPI
    return root, s * p


def ntk(gram, ur, uc, scale):
    t = gram * (ur * uc)
    root, w = half_angle(jnp.abs(t))
    h = jnp.where(t < 0.0, w, 1.0 - w)
    th = t * h
    jf = root + th
    theta = th + jf
    root2, w2 = half_angle(jnp.minimum(jf, 1.0))
    h2 = 1.0 - w2
    return (root2 + h2 * (theta + jf)) * scale


def squares(x):
    x = x.astype(F32)
    return split(x * x)


def col_form(sq):
    ones = jnp.ones((128, F), BF)
    return (dot(sq[0], ones, NT) + dot(sq[1], ones, NT)) * (1.0 / F) + 1e-6


def row_form(sq):
    ones = jnp.ones((8, F), BF)
    return (dot(ones, sq[0], NT) + dot(ones, sq[1], NT))[0:1] * (1.0 / F) + 1e-6


def full_kernel(B, R, C, Q, out_l, out_t, xr, xc, xp, qr, qc, qcr, qpr, qpc, M, kr, kc, oslot, osem):
    r = lax.axis_index("row")
    z = lax.axis_index("col")
    N = 256
    for t in range(2):
        v = Q[t].reshape(128, F)
        xp[t * 128:(t + 1) * 128] = v
        sq = squares(v)
        qpc[t * 128:(t + 1) * 128] = col_form(sq)
        qpr[:, t * 128:(t + 1) * 128] = row_form(sq)
    for a in range(3):
        v = R[:, a].reshape(128, F)
        xr[a * 128:(a + 1) * 128] = v
        qr[a * 128:(a + 1) * 128] = col_form(squares(v))
        for b in range(2):
            t = 2 * a + b
            v = C[b, :, a].reshape(128, F)
            xc[t * 128:(t + 1) * 128] = v
            sq = squares(v)
            qc[t * 128:(t + 1) * 128] = col_form(sq)
            qcr[:, t * 128:(t + 1) * 128] = row_form(sq)
    ii = lax.broadcasted_iota(jnp.int32, (128, 128), 0)
    jj = lax.broadcasted_iota(jnp.int32, (128, 128), 1)

    def tile(xa, qa, xb, qb, same):
        gram = dot(xa, xb, NT) * (1.0 / F)
        k = ntk(gram, lax.rsqrt(qa), lax.rsqrt(qb), jnp.sqrt(qa) * jnp.sqrt(qb))
        if same is False:
            return k
        eq = ii == jj if same is True else (ii == jj) & same
        return jnp.where(eq, gram + 2.0 * qa + 1.0, k)

    def at(ref, i):
        return ref[pl.ds(pl.multiple_of(i * 128, 128), 128)]

    for i in range(2):
        for t in range(2):
            M[i * 128:(i + 1) * 128, t * 128:(t + 1) * 128] = tile(
                at(xp, i), at(qpc, i), at(xp, t), qpr[:, t * 128:(t + 1) * 128], i == t)
    ri = lax.broadcasted_iota(jnp.int32, (N, N), 0)
    ci = lax.broadcasted_iota(jnp.int32, (N, N), 1)
    M[:, N:2 * N] = jnp.where(ri == ci, 1.0, 0.0)

    bi = lax.broadcasted_iota(jnp.int32, (B, B), 0)
    bj = lax.broadcasted_iota(jnp.int32, (B, B), 1)
    b2i = lax.broadcasted_iota(jnp.int32, (B, 2 * B), 0)
    for n in range(N // B):
        lo = n * B
        S = jnp.concatenate([M[lo:lo + B, lo:lo + B], jnp.where(bi == bj, 1.0, 0.0)], axis=1)
        dinv = jnp.zeros((B, 1), F32)
        for j in range(B):
            d = lax.rsqrt(S[j:j + 1, j:j + 1])
            row = S[j:j + 1, :] * d
            colv = S[:, j:j + 1] * d
            below = b2i > j
            S = jnp.where(below, S - colv * row, jnp.where(b2i == j, row, S))
        w = split(S[:, B:])
        Y = dot3(w, split(M[lo:lo + B, :]), NN)
        M[lo:lo + B, :] = Y
        if lo + B < N:
            ys = split(Y)
            U = split(Y[:, lo + B:N])
            M[lo + B:, lo + B:] = M[lo + B:, lo + B:] - dot3(U, tuple(v[:, lo + B:] for v in ys), TN)
    w = split(M[:, N:])

    for i in range(3):
        for t in range(2):
            kr[i * 128:(i + 1) * 128, t * 128:(t + 1) * 128] = tile(
                at(xr, i), at(qr, i), at(xp, t), qpr[:, t * 128:(t + 1) * 128],
                (r == t) if i == 0 else False)
    for i in range(6):
        for t in range(2):
            kc[i * 128:(i + 1) * 128, t * 128:(t + 1) * 128] = tile(
                at(xc, i), at(qc, i), at(xp, t), qpr[:, t * 128:(t + 1) * 128],
                (z == t) if i == 0 else False)
    lr = dot3(split(kr[...]), w, NT)
    out_l[...] = lr
    lc = dot3(split(kc[...]), w, NT)
    lr = split(lr)
    lc = split(lc)
    for a in range(3):
        rows = slice(a * 128, (a + 1) * 128)
        for t in range(6):
            cols = slice(t * 128, (t + 1) * 128)
            b = t % 2
            k = tile(at(xr, a), at(qr, a), at(xc, t), qcr[:, cols],
                     (r == z + 16 * b) if t // 2 == a else False)
            k = k - dot3(tuple(v[rows] for v in lr), tuple(v[cols] for v in lc), NT)
            oslot[t, rows] = k
    copies = []
    for a in range(3):
        for t in range(6):
            c = pltpu.make_async_copy(oslot.at[t, pl.ds(a * 128, 128)], out_t.at[a, 0, :, t, 0, :], osem.at[a, t])
            c.start()
            copies.append(c)
    for c in copies:
        c.wait()


def compute(R, C, Q, B=32, interpret=False):
    vm = pl.BlockSpec(memory_space=pltpu.VMEM)
    out_l, out_t = pl.pallas_call(
        functools.partial(full_kernel, B),
        out_shape=(jax.ShapeDtypeStruct((384, 256), F32),
                   jax.ShapeDtypeStruct((3, 1, 128, 6, 1, 128), F32)),
        in_specs=[vm] * 3,
        out_specs=(vm, pl.BlockSpec(memory_space=pl.ANY)),
        scratch_shapes=[pltpu.VMEM((384, F), BF), pltpu.VMEM((768, F), BF), pltpu.VMEM((256, F), BF),
                        pltpu.VMEM((384, 128), F32), pltpu.VMEM((768, 128), F32), pltpu.VMEM((1, 768), F32),
                        pltpu.VMEM((1, 256), F32), pltpu.VMEM((256, 128), F32), pltpu.VMEM((256, 512), F32),
                        pltpu.VMEM((384, 256), F32), pltpu.VMEM((768, 256), F32), pltpu.VMEM((6, 384, 128), F32),
                        pltpu.SemaphoreType.DMA((3, 6))],
        name="panel_kernel", interpret=interpret,
    )(R, C, Q)
    return out_l.reshape(3, 1, 128, 256), out_t


def local(features):
    R, C, Q = gather(features, 2)
    return compute(R, C, Q, 32)


def solution(mesh):
    return jax.shard_map(
        local,
        mesh=mesh,
        in_specs=(P(None, "row", "col", None),),
        out_specs=(P(None, "row", None, None), P(None, "row", None, None, "col", None)),
        check_vma=False,
    )
```

```python
import functools, math
import jax, jax.numpy as jnp
from jax import lax
from jax.experimental import pallas as pl
from jax.experimental.pallas import tpu as pltpu
from jax.sharding import PartitionSpec as P
MESH = pl.DeviceIdType.MESH
NZ = 16

def comm_kernel(H, x_ref, R, C, Q, lsem, zrecv, zsend, crecv, csend, qrecv, qsend, lc_sem):
    r = lax.axis_index("row")
    z = lax.axis_index("col")
    core = r % 2
    y = (r // 2) % 4
    x = r // 8

    def rid(xx, yy, cc):
        return (((xx + 4) % 4) * 4 + ((yy + 4) % 4)) * 2 + cc

    own = pltpu.make_async_copy(x_ref.at[:, 0], R.at[z], lsem)
    own.start()
    bar = pltpu.get_barrier_semaphore()
    peers = []
    zs = [j for j in range(1, H + 1)] + [16 - j for j in range(1, H + 1)]
    for j in sorted(set(zs)):
        peers.append((r, (z + j) % 16))
    for j in (1, 2, 3):
        peers.append((rid(x, y + j, core), z))
        peers.append((rid(x + j, y, core), z))
    peers.append((rid(x, y, 1 - core), z))
    for p in peers:
        pl.semaphore_signal(bar, inc=1, device_id=p, device_id_type=MESH)
    pl.semaphore_wait(bar, len(peers))
    own.wait()

    def zcopy(o, d, j):
        return pltpu.make_async_remote_copy(
            src_ref=R.at[o], dst_ref=R.at[o], send_sem=zsend.at[(0 if d > 0 else H) + j - 1],
            recv_sem=zrecv.at[o], device_id=(r, (z + d * j + 16) % 16), device_id_type=MESH)

    xs0, ys, cs = z // 8, (z // 2) % 4, z % 2
    streams = []
    for t in range(2):
        streams.append((qrecv, qsend, t, Q, 0, 0, t))
    for b in range(2):
        streams.append((crecv, csend, b, C, xs0 + 2 * b, ys, cs))

    def targets():
        ts = [(rid(x, y + j, core), z) for j in (1, 2, 3)]
        ts += [(rid(x + j, y, core), z) for j in (1, 2, 3)]
        ts += [(rid(x, y, 1 - core), z)]
        return ts

    def src_of(S, o):
        rs, ss, i, buf, rx, ry, rc = S
        return R.at[o, 0] if buf is Q else R.at[o]

    def pcopy(S, o, k, src):
        rs, ss, i, buf, rx, ry, rc = S
        return pltpu.make_async_remote_copy(
            src_ref=src, dst_ref=buf.at[i, o], send_sem=ss.at[i, k], recv_sem=rs.at[i, o],
            device_id=targets()[k], device_id_type=MESH)

    def roles(S):
        rs, ss, i, buf, rx, ry, rc = S
        oncore = core == rc
        is_src = oncore & (x == rx) & (y == ry)
        is_y = oncore & (x == rx) & (y != ry)
        is_x = oncore & (x != rx)
        is_s = core != rc
        return is_src, is_y, is_x, is_s

    def local_copy(S, o):
        rs, ss, i, buf, rx, ry, rc = S
        return pltpu.make_async_copy(src_of(S, o), buf.at[i, o], rs.at[i, o])

    def at_source(o):
        for S in streams:
            @pl.when(roles(S)[0])
            def _():
                for k in range(7):
                    pcopy(S, o, k, src_of(S, o)).start()
                local_copy(S, o).start()

    def wait_block(S, o):
        rs, ss, i, buf, rx, ry, rc = S
        pltpu.make_async_copy(buf.at[i, o], buf.at[i, o], rs.at[i, o]).wait()

    def relay(which, o):
        for S in streams:
            role = roles(S)[which]
            buf, i = S[3], S[2]
            @pl.when(role)
            def _():
                wait_block(S, o)
                ks = {1: (3, 4, 5, 6), 2: (6,), 3: ()}[which]
                for k in ks:
                    pcopy(S, o, k, buf.at[i, o]).start()

    for j in range(1, H + 1):
        zcopy(z, 1, j).start()
        if j <= 7:
            zcopy(z, -1, j).start()
    at_source(z)

    def seq(i):
        d = (i + 1) // 2
        return lax.rem(jnp.where(i % 2 == 1, z - d, z + d) + 16, 16)

    def step(i, _):
        @pl.when((i >= 1) & (i < 16))
        def _():
            o = seq(i)
            d = (i + 1) // 2
            pltpu.make_async_copy(R.at[o], R.at[o], zrecv.at[o]).wait()
            fwd = (d % H == 0)
            @pl.when(fwd & (i % 2 == 1))
            def _():
                for j in range(1, H + 1):
                    @pl.when(d + j <= 8)
                    def _():
                        zcopy(o, 1, j).start()
            @pl.when(fwd & (i % 2 == 0))
            def _():
                for j in range(1, min(H, 7) + 1):
                    @pl.when(d + j <= 7)
                    def _():
                        zcopy(o, -1, j).start()
            at_source(o)
        for which, lag in ((1, 2), (2, 4), (3, 5)):
            @pl.when((i >= lag) & (i < 16 + lag))
            def _():
                relay(which, seq(i - lag))
        return 0

    lax.fori_loop(0, 21, step, 0)

    for S in streams:
        @pl.when(roles(S)[0])
        def _():
            def w(o, _):
                wait_block(S, o)
                return 0
            lax.fori_loop(0, 16, w, 0)
    for d, lim in ((1, 8), (-1, 7)):
        for j in range(1, H + 1):
            n = (1 if j <= lim else 0) + sum(1 for dd in range(H, lim, H) if dd + j <= lim)
            if n:
                v = R.at[pl.ds(0, n)]
                pltpu.make_async_copy(v, v, zsend.at[(0 if d > 0 else H) + j - 1]).wait()
    for S in streams:
        rs, ss, i, buf, rx, ry, rc = S
        is_src, is_y, is_x, is_s = roles(S)
        for k in range(7):
            cond = is_src if k < 3 else ((is_src | is_y) if k < 6 else (core == rc))
            @pl.when(cond)
            def _():
                pltpu.make_async_copy(buf.at[i], buf.at[i], ss.at[i, k]).wait()


def gather(features, H=1):
    vm = pl.BlockSpec(memory_space=pltpu.VMEM)
    return pl.pallas_call(
        functools.partial(comm_kernel, H),
        out_shape=(jax.ShapeDtypeStruct((16, 3, 8, 512), jnp.bfloat16),
                   jax.ShapeDtypeStruct((2, 16, 3, 8, 512), jnp.bfloat16),
                   jax.ShapeDtypeStruct((2, 16, 8, 512), jnp.bfloat16)),
        in_specs=[pl.BlockSpec(memory_space=pl.ANY)],
        out_specs=(vm, vm, vm),
        scratch_shapes=[pltpu.SemaphoreType.DMA, pltpu.SemaphoreType.DMA((16,)), pltpu.SemaphoreType.DMA((2 * H,)),
                        pltpu.SemaphoreType.DMA((2, 16)), pltpu.SemaphoreType.DMA((2, 7)),
                        pltpu.SemaphoreType.DMA((2, 16)), pltpu.SemaphoreType.DMA((2, 7)),
                        pltpu.SemaphoreType.DMA],
        compiler_params=pltpu.CompilerParams(collective_id=0, has_side_effects=True),
        name="gather_features",
    )(features)


F = 512
F32 = jnp.float32
BF = jnp.bfloat16
IPI = 1.0 / math.pi
POLY = (1.5707963050, -0.2145988016, 0.0889789874, -0.0501743046,
        0.0308918810, -0.0170881256, 0.0066700901, -0.0012624911)
NT = (((1,), (1,)), ((), ()))
NN = (((1,), (0,)), ((), ()))
TN = (((0,), (0,)), ((), ()))


def dot(a, b, dims):
    return lax.dot_general(a, b, dims, preferred_element_type=F32)


def split(a):
    hi = a.astype(BF)
    return hi, (a - hi.astype(F32)).astype(BF)


def dot3(a, b, dims):
    return dot(a[0], b[0], dims) + (dot(a[0], b[1], dims) + dot(a[1], b[0], dims))


def half_angle(ax):
    y = jnp.maximum(1.0 - ax, 1e-30)
    s = y * lax.rsqrt(y)
    z = 1.0 + ax
    root = (s * IPI) * (z * lax.rsqrt(z))
    p = POLY[7] * IPI
    for c in POLY[6::-1]:
        p = p * ax + c * IPI
    return root, s * p


def ntk(gram, ur, uc, scale):
    t = gram * (ur * uc)
    root, w = half_angle(jnp.abs(t))
    h = jnp.where(t < 0.0, w, 1.0 - w)
    th = t * h
    jf = root + th
    theta = th + jf
    root2, w2 = half_angle(jnp.minimum(jf, 1.0))
    h2 = 1.0 - w2
    return (root2 + h2 * (theta + jf)) * scale


def squares(x):
    x = x.astype(F32)
    return split(x * x)


def col_form(sq):
    ones = jnp.ones((128, F), BF)
    return (dot(sq[0], ones, NT) + dot(sq[1], ones, NT)) * (1.0 / F) + 1e-6


def row_form(sq):
    ones = jnp.ones((8, F), BF)
    return (dot(ones, sq[0], NT) + dot(ones, sq[1], NT))[0:1] * (1.0 / F) + 1e-6


def full_kernel(B, skip, R, C, Q, out_l, out_t, xr, xc, xp, qr, qc, qcr, qpr, qpc, M, kr, kc, oslot, osem):
    r = lax.axis_index("row")
    z = lax.axis_index("col")
    N = 256
    for t in range(2):
        v = Q[t].reshape(128, F)
        xp[t * 128:(t + 1) * 128] = v
        sq = squares(v)
        qpc[t * 128:(t + 1) * 128] = col_form(sq)
        qpr[:, t * 128:(t + 1) * 128] = row_form(sq)
    for a in range(3):
        v = R[:, a].reshape(128, F)
        xr[a * 128:(a + 1) * 128] = v
        qr[a * 128:(a + 1) * 128] = col_form(squares(v))
        for b in range(2):
            t = 2 * a + b
            v = C[b, :, a].reshape(128, F)
            xc[t * 128:(t + 1) * 128] = v
            sq = squares(v)
            qc[t * 128:(t + 1) * 128] = col_form(sq)
            qcr[:, t * 128:(t + 1) * 128] = row_form(sq)
    ii = lax.broadcasted_iota(jnp.int32, (128, 128), 0)
    jj = lax.broadcasted_iota(jnp.int32, (128, 128), 1)

    def tile(xa, qa, xb, qb, same):
        gram = dot(xa, xb, NT) * (1.0 / F)
        k = ntk(gram, lax.rsqrt(qa), lax.rsqrt(qb), jnp.sqrt(qa) * jnp.sqrt(qb))
        if same is False:
            return k
        eq = ii == jj if same is True else (ii == jj) & same
        return jnp.where(eq, gram + 2.0 * qa + 1.0, k)

    def at(ref, i):
        return ref[pl.ds(pl.multiple_of(i * 128, 128), 128)]

    for i in range(2):
        for t in range(2):
            M[i * 128:(i + 1) * 128, t * 128:(t + 1) * 128] = tile(
                at(xp, i), at(qpc, i), at(xp, t), qpr[:, t * 128:(t + 1) * 128], i == t)
    ri = lax.broadcasted_iota(jnp.int32, (N, N), 0)
    ci = lax.broadcasted_iota(jnp.int32, (N, N), 1)
    M[:, N:2 * N] = jnp.where(ri == ci, 1.0, 0.0)

    sub = lax.broadcasted_iota(jnp.int32, (8, 128), 0)
    G = B // 8

    def wide(v):
        return jnp.broadcast_to(v, (8, 128))

    for n in range(0 if 'C' in skip else N // B):
        lo = n * B
        hi = lo + B
        D = M[lo:hi, lo // 128 * 128:lo // 128 * 128 + 128]
        o = lo % 128
        col = [[wide(D[8 * g:8 * g + 8, o + k:o + k + 1]) if g >= k // 8 else None for g in range(G)]
               for k in range(B)]
        lanes = list(range(hi // 128, 2)) + list(range(2, 3 + (hi - 1) // 128))
        S = [[M[lo + 8 * g:lo + 8 * g + 8, 128 * v:128 * v + 128] for v in lanes] for g in range(G)]
        for k in range(0 if 'c' in skip else B):
            gk = k // 8
            rs = wide(lax.rsqrt(col[k][gk])[k % 8:k % 8 + 1])
            c = [col[k][g] * rs if g >= gk else None for g in range(G)]
            for m in range(k + 1, B):
                f = wide(c[m // 8][m % 8:m % 8 + 1])
                for g in range(m // 8, G):
                    col[m][g] = col[m][g] - c[g] * f
            below = jnp.where(sub > k % 8, c[gk], 0.0)
            for v in range(len(lanes)):
                row = wide(S[gk][v][k % 8:k % 8 + 1]) * rs
                S[gk][v] = jnp.where(sub == k % 8, row, S[gk][v] - below * row)
                for g in range(gk + 1, G):
                    S[g][v] = S[g][v] - c[g] * row
        Y = [jnp.concatenate([S[g][v] for g in range(G)], axis=0) for v in range(len(lanes))]
        for v in range(len(lanes)):
            M[lo:hi, 128 * lanes[v]:128 * lanes[v] + 128] = Y[v]
        if hi < N:
            ys = [split(y) for y in Y]
            U = split(M[lo:hi, hi:N])
            for v in range(len(lanes)):
                cs = slice(128 * lanes[v], 128 * lanes[v] + 128)
                M[hi:, cs] = M[hi:, cs] - dot3(U, ys[v], TN)
    w = split(M[:, N:])

    for i in range(0 if 'k' in skip else 3):
        for t in range(2):
            kr[i * 128:(i + 1) * 128, t * 128:(t + 1) * 128] = tile(
                at(xr, i), at(qr, i), at(xp, t), qpr[:, t * 128:(t + 1) * 128],
                (r == t) if i == 0 else False)
    for i in range(0 if 'k' in skip else 6):
        for t in range(2):
            kc[i * 128:(i + 1) * 128, t * 128:(t + 1) * 128] = tile(
                at(xc, i), at(qc, i), at(xp, t), qpr[:, t * 128:(t + 1) * 128],
                (z == t) if i == 0 else False)
    lr = dot3(split(kr[...]), w, NT)
    out_l[...] = lr
    lc = dot3(split(kc[...]), w, NT)
    lr = split(lr)
    lc = split(lc)
    copies = []
    for a in range(0 if 't' in skip else 3):
        rows = slice(a * 128, (a + 1) * 128)
        for t in range(6):
            cols = slice(t * 128, (t + 1) * 128)
            b = t % 2
            k = tile(at(xr, a), at(qr, a), at(xc, t), qcr[:, cols],
                     (r == z + 16 * b) if t // 2 == a else False)
            k = k - dot3(tuple(v[rows] for v in lr), tuple(v[cols] for v in lc), NT)
            oslot[pl.ds(a * 768 + t, 128, stride=6), :] = k
        c = pltpu.make_async_copy(oslot.at[pl.ds(a * 768, 768)], out_t.at[pl.ds(a * 768, 768)], osem.at[a])
        c.start()
        copies.append(c)
    for c in copies:
        c.wait()


def compute(R, C, Q, B=32, interpret=False, skip=''):
    vm = pl.BlockSpec(memory_space=pltpu.VMEM)
    out_l, out_t = pl.pallas_call(
        functools.partial(full_kernel, B, skip),
        out_shape=(jax.ShapeDtypeStruct((384, 256), F32),
                   jax.ShapeDtypeStruct((2304, 128), F32)),
        in_specs=[vm] * 3,
        out_specs=(vm, pl.BlockSpec(memory_space=pl.ANY)),
        scratch_shapes=[pltpu.VMEM((384, F), BF), pltpu.VMEM((768, F), BF), pltpu.VMEM((256, F), BF),
                        pltpu.VMEM((384, 128), F32), pltpu.VMEM((768, 128), F32), pltpu.VMEM((1, 768), F32),
                        pltpu.VMEM((1, 256), F32), pltpu.VMEM((256, 128), F32), pltpu.VMEM((256, 512), F32),
                        pltpu.VMEM((384, 256), F32), pltpu.VMEM((768, 256), F32), pltpu.VMEM((2304, 128), F32),
                        pltpu.SemaphoreType.DMA((3,))],
        name="panel_kernel", interpret=interpret,
    )(R, C, Q)
    return out_l.reshape(3, 1, 128, 256), out_t.reshape(3, 1, 128, 6, 1, 128)


def local(features):
    R, C, Q = gather(features, 2)
    return compute(R, C, Q, 32)


def solution(mesh):
    return jax.shard_map(
        local,
        mesh=mesh,
        in_specs=(P(None, "row", "col", None),),
        out_specs=(P(None, "row", None, None), P(None, "row", None, None, "col", None)),
        check_vma=False,
    )
```

```python
import functools
import math

import jax
import jax.numpy as jnp
from jax import lax
from jax.experimental import pallas as pl
from jax.experimental.pallas import tpu as pltpu
from jax.sharding import PartitionSpec as P

MESH = pl.DeviceIdType.MESH

F = 512
F32 = jnp.float32
BF = jnp.bfloat16
IPI = 1.0 / math.pi
POLY = (1.5707963050, -0.2145988016, 0.0889789874, -0.0501743046,
        0.0308918810, -0.0170881256, 0.0066700901, -0.0012624911)
NT = (((1,), (1,)), ((), ()))
NN = (((1,), (0,)), ((), ()))
TN = (((0,), (0,)), ((), ()))


def dot(a, b, dims):
    return lax.dot_general(a, b, dims, preferred_element_type=F32)


def split(a):
    hi = a.astype(BF)
    return hi, (a - hi.astype(F32)).astype(BF)


def dot3(a, b, dims):
    return dot(a[0], b[0], dims) + (dot(a[0], b[1], dims) + dot(a[1], b[0], dims))


def half_angle(ax):
    y = jnp.maximum(1.0 - ax, 1e-30)
    s = y * lax.rsqrt(y)
    z = 1.0 + ax
    root = (s * IPI) * (z * lax.rsqrt(z))
    p = POLY[7] * IPI
    for c in POLY[6::-1]:
        p = p * ax + c * IPI
    return root, s * p


def ntk(gram, ur, uc, scale):
    t = gram * (ur * uc)
    root, w = half_angle(jnp.abs(t))
    h = jnp.where(t < 0.0, w, 1.0 - w)
    th = t * h
    jf = root + th
    theta = th + jf
    root2, w2 = half_angle(jnp.minimum(jf, 1.0))
    h2 = 1.0 - w2
    return (root2 + h2 * (theta + jf)) * scale


def squares(x):
    x = x.astype(F32)
    return split(x * x)


def col_form(sq):
    ones = jnp.ones((128, F), BF)
    return (dot(sq[0], ones, NT) + dot(sq[1], ones, NT)) * (1.0 / F) + 1e-6


def row_form(sq):
    ones = jnp.ones((8, F), BF)
    return (dot(ones, sq[0], NT) + dot(ones, sq[1], NT))[0:1] * (1.0 / F) + 1e-6


VLIM = 24 * 1024 * 1024


def at(ref, i):
    return ref[i * 128:(i + 1) * 128]


def tile(xa, qa, xb, qb, same):
    gram = dot(xa, xb, NT) * (1.0 / F)
    k = ntk(gram, lax.rsqrt(qa), lax.rsqrt(qb), jnp.sqrt(qa) * jnp.sqrt(qb))
    if same is False:
        return k
    ii = lax.broadcasted_iota(jnp.int32, (128, 128), 0)
    jj = lax.broadcasted_iota(jnp.int32, (128, 128), 1)
    eq = ii == jj if same is True else (ii == jj) & same
    return jnp.where(eq, gram + 2.0 * qa + 1.0, k)


NZ = 16
PANEL0 = 3
RING2, ROOT, RING4 = 9, 12, 18
LOOP = PANEL0 + NZ


def panel_kernel(B, x_ref, C, R, xp, qpr, w_hi, w_lo, Q, qpc, M,
                 lsem, zrecv, zsend, crecv, csend, cdir, qrecv, qplane, qz, qsib):
    r = lax.axis_index("row")
    z = lax.axis_index("col")
    core = r % 2
    y = (r // 2) % 4
    x = r // 8
    N = 256
    is_root = (x == 0) & (y == 0)

    def rid(xx, yy, cc):
        return (((xx + 4) % 4) * 4 + ((yy + 4) % 4)) * 2 + cc

    own = pltpu.make_async_copy(x_ref.at[:, 0], R.at[z], lsem)
    own.start()
    sibling = (r + 1 - 2 * core, z)
    others = [((r + k) % 32, z) for k in range(1, 32)]
    to_root = (2 * z + r // NZ, r % NZ)
    cb, co = core, r // 2
    from_z = (z + NZ * core, r // 2)
    alone = (to_root[0] == r) & (to_root[1] == z)

    plane = [(rid(x + k // 4, y + k % 4, core), z) for k in (10, 6, 14, 9, 11, 2, 8, 5, 7, 13, 15, 1, 3, 4, 12)]
    bar = pltpu.get_barrier_semaphore()

    def hello(p):
        pl.semaphore_signal(bar, inc=1, device_id=p, device_id_type=MESH)

    for p in [(r, (z + k) % NZ) for k in range(1, NZ)] + others:
        hello(p)

    @pl.when(alone)
    def _():
        pl.semaphore_wait(bar, NZ - 1 + 31)

    @pl.when(jnp.logical_not(alone))
    def _():
        hello(to_root)
        hello(from_z)
        pl.semaphore_wait(bar, NZ - 1 + 31 + 2)

    own.wait()

    def remote(src, dst, ssem, rsem, to):
        return pltpu.make_async_remote_copy(src_ref=src, dst_ref=dst, send_sem=ssem, recv_sem=rsem,
                                            device_id=to, device_id_type=MESH)

    mine = Q.at[core, z]

    @pl.when(is_root)
    def _():
        for k in range(15):
            remote(R.at[z, 0], mine, qplane.at[k], qrecv.at[core, z], plane[k]).start()
        pltpu.make_async_copy(R.at[z, 0], mine, qrecv.at[core, z]).start()

    @pl.when(alone)
    def _():
        pltpu.make_async_copy(R.at[z], C.at[r // NZ, z], crecv.at[r // NZ, z]).start()

    @pl.when(jnp.logical_not(alone))
    def _():
        remote(R.at[z], C.at[r // NZ, z], cdir, crecv.at[r // NZ, z], to_root).start()

    def zcopy(o, d, hops):
        return remote(R.at[o], R.at[o], zsend.at[(0 if d > 0 else 2) + hops - 1], zrecv.at[o],
                      (r, (z + d * hops + NZ) % NZ))

    def qwait(t, o):
        pltpu.make_async_copy(Q.at[t, o], Q.at[t, o], qrecv.at[t, o]).wait()

    def to_sibling(o):
        remote(Q.at[core, o], Q.at[core, o], qsib, qrecv.at[core, o], sibling).start()

    qwait(core, z)
    for k in (8, 7, 9, 6, 10, 5, 11, 4, 12, 3, 13, 2, 14, 1, 15):
        remote(mine, mine, qz.at[k - 1], qrecv.at[core, z], (r, (z + k) % NZ)).start()
    to_sibling(z)
    for hops in (2, 1):
        zcopy(z, 1, hops).start()
        zcopy(z, -1, hops).start()

    def seq(i):
        d = (i + 1) // 2
        return lax.rem(jnp.where(i % 2 == 1, z - d, z + d) + NZ, NZ)

    def panel_step(tau):
        i = tau - PANEL0

        @pl.when((i >= 1) & (i < NZ))
        def _():
            o = seq(i)
            qwait(core, o)
            to_sibling(o)

    def arrived(o):
        pltpu.make_async_copy(R.at[o], R.at[o], zrecv.at[o]).wait()

    def along_z(d):
        up, down = (z - d + NZ) % NZ, (z + d) % NZ
        arrived(up)
        if d < 8:
            zcopy(up, 1, 2).start()
            zcopy(up, 1, 1).start()
            arrived(down)
            if d < 6:
                zcopy(down, -1, 2).start()
            zcopy(down, -1, 1).start()
        arrived((z - d + 1 + NZ) % NZ)
        arrived((z + d - 1) % NZ)

    blk = C.at[cb, co]

    def cwait(b, o):
        pltpu.make_async_copy(C.at[b, o], C.at[b, o], crecv.at[b, o]).wait()

    def step(tau, carry):
        panel_step(tau)

        @pl.when(tau == RING2)
        def _():
            along_z(2)

        @pl.when(tau == ROOT)
        def _():
            cwait(cb, co)
            for k in range(31):
                remote(blk, blk, csend.at[k], crecv.at[cb, co], others[k]).start()

        @pl.when(tau == RING4)
        def _():
            along_z(4)

        return carry

    lax.fori_loop(0, LOOP, step, 0)

    def from_sibling(o, carry):
        qwait(1 - core, o)
        return carry

    lax.fori_loop(0, NZ, from_sibling, 0)

    for t in range(2):
        v = Q[t].reshape(128, F)
        xp[t * 128:(t + 1) * 128] = v
        sq = squares(v)
        qpc[t * 128:(t + 1) * 128] = col_form(sq)
        qpr[:, t * 128:(t + 1) * 128] = row_form(sq)

    for i in range(2):
        for t in range(2):
            M[i * 128:(i + 1) * 128, t * 128:(t + 1) * 128] = tile(
                at(xp, i), at(qpc, i), at(xp, t), qpr[:, t * 128:(t + 1) * 128], i == t)
    ri = lax.broadcasted_iota(jnp.int32, (N, N), 0)
    ci = lax.broadcasted_iota(jnp.int32, (N, N), 1)
    M[:, N:2 * N] = jnp.where(ri == ci, 1.0, 0.0)

    def after_block(n):
        if n == 2:
            along_z(6)
        if n == 6:
            along_z(8)

    sub = lax.broadcasted_iota(jnp.int32, (8, 128), 0)
    G = B // 8

    def wide(v):
        return jnp.broadcast_to(v, (8, 128))

    for n in range(N // B):
        lo = n * B
        hi = lo + B
        D = M[lo:hi, lo // 128 * 128:lo // 128 * 128 + 128]
        o = lo % 128
        col = [[wide(D[8 * g:8 * g + 8, o + k:o + k + 1]) if g >= k // 8 else None for g in range(G)]
               for k in range(B)]
        lanes = list(range(hi // 128, 2)) + list(range(2, 3 + (hi - 1) // 128))
        S = [[M[lo + 8 * g:lo + 8 * g + 8, 128 * v:128 * v + 128] for v in lanes] for g in range(G)]
        for k in range(B):
            gk = k // 8
            rs = wide(lax.rsqrt(col[k][gk])[k % 8:k % 8 + 1])
            c = [col[k][g] * rs if g >= gk else None for g in range(G)]
            for m in range(k + 1, B):
                f = wide(c[m // 8][m % 8:m % 8 + 1])
                for g in range(m // 8, G):
                    col[m][g] = col[m][g] - c[g] * f
            below = jnp.where(sub > k % 8, c[gk], 0.0)
            for v in range(len(lanes)):
                row = wide(S[gk][v][k % 8:k % 8 + 1]) * rs
                S[gk][v] = jnp.where(sub == k % 8, row, S[gk][v] - below * row)
                for g in range(gk + 1, G):
                    S[g][v] = S[g][v] - c[g] * row
        Y = [jnp.concatenate([S[g][v] for g in range(G)], axis=0) for v in range(len(lanes))]
        for v in range(len(lanes)):
            M[lo:hi, 128 * lanes[v]:128 * lanes[v] + 128] = Y[v]
        if hi < N:
            ys = [split(y) for y in Y]
            U = split(M[lo:hi, hi:N])
            for v in range(len(lanes)):
                cs = slice(128 * lanes[v], 128 * lanes[v] + 128)
                M[hi:, cs] = M[hi:, cs] - dot3(U, ys[v], TN)
        after_block(n)
    wf = split(M[:, N:])
    w_hi[...] = wf[0]
    w_lo[...] = wf[1]

    def sent(ref, sem):
        pltpu.make_async_copy(ref, ref, sem).wait()

    @pl.when(is_root)
    def _():
        for k in range(15):
            sent(mine, qplane.at[k])

    for k in range(15):
        sent(mine, qz.at[k])
    sent(Q.at[0], qsib)

    @pl.when(jnp.logical_not(alone))
    def _():
        sent(R.at[0], cdir)

    for k, n in ((0, 4), (1, 4), (2, 4), (3, 3)):
        sent(R.at[pl.ds(0, n)], zsend.at[k])
    for k in range(31):
        sent(blk, csend.at[k])

    def rest(o, carry):
        cwait(1 - cb, o)

        @pl.when(o != co)
        def _():
            cwait(cb, o)
        return carry

    lax.fori_loop(0, NZ, rest, 0)


def update_kernel(C, R, xp, qpr, w_hi, w_lo, out_l, out_t, xr, qr, kr, xc, qc, qcr, kc, oslot, osem):
    r = lax.axis_index("row")
    z = lax.axis_index("col")
    w = (w_hi[...], w_lo[...])
    for a in range(3):
        v = R[:, a].reshape(128, F)
        xr[a * 128:(a + 1) * 128] = v
        qr[a * 128:(a + 1) * 128] = col_form(squares(v))
        for t in range(2):
            kr[a * 128:(a + 1) * 128, t * 128:(t + 1) * 128] = tile(
                at(xr, a), at(qr, a), at(xp, t), qpr[:, t * 128:(t + 1) * 128], (r == t) if a == 0 else False)
    lr = dot3(split(kr[...]), w, NT)
    out_l[...] = lr
    for a in range(3):
        for b in range(2):
            t = 2 * a + b
            v = C[b, :, a].reshape(128, F)
            xc[t * 128:(t + 1) * 128] = v
            sq = squares(v)
            qc[t * 128:(t + 1) * 128] = col_form(sq)
            qcr[:, t * 128:(t + 1) * 128] = row_form(sq)
    for i in range(6):
        for t in range(2):
            kc[i * 128:(i + 1) * 128, t * 128:(t + 1) * 128] = tile(
                at(xc, i), at(qc, i), at(xp, t), qpr[:, t * 128:(t + 1) * 128],
                (z == t) if i == 0 else False)
    lc = split(dot3(split(kc[...]), w, NT))
    lr = split(lr)
    copies = []
    for a in range(3):
        rows = slice(a * 128, (a + 1) * 128)
        for t in range(6):
            cols = slice(t * 128, (t + 1) * 128)
            k = tile(at(xr, a), at(qr, a), at(xc, t), qcr[:, cols],
                     (r == z + NZ * (t % 2)) if t // 2 == a else False)
            k = k - dot3(tuple(v[rows] for v in lr), tuple(v[cols] for v in lc), NT)
            oslot[pl.ds(a * 768 + t, 128, stride=6), :] = k
        c = pltpu.make_async_copy(oslot.at[pl.ds(a * 768, 768)], out_t.at[pl.ds(a * 768, 768)], osem.at[a])
        c.start()
        copies.append(c)
    for c in copies:
        c.wait()


def local(features):
    dma = pltpu.SemaphoreType.DMA
    vm = pl.BlockSpec(memory_space=pltpu.VMEM)
    parts = pl.pallas_call(
        functools.partial(panel_kernel, 32),
        out_shape=(jax.ShapeDtypeStruct((2, NZ, 3, 8, F), BF), jax.ShapeDtypeStruct((NZ, 3, 8, F), BF),
                   jax.ShapeDtypeStruct((256, F), BF), jax.ShapeDtypeStruct((1, 256), F32),
                   jax.ShapeDtypeStruct((256, 256), BF), jax.ShapeDtypeStruct((256, 256), BF)),
        in_specs=[pl.BlockSpec(memory_space=pl.ANY)],
        out_specs=(vm,) * 6,
        scratch_shapes=[pltpu.VMEM((2, NZ, 8, F), BF),
                        pltpu.VMEM((256, 128), F32), pltpu.VMEM((256, 512), F32),
                        dma, dma((NZ,)), dma((4,)), dma((2, NZ)), dma((31,)), dma,
                        dma((2, NZ)), dma((15,)), dma((15,)), dma],
        compiler_params=pltpu.CompilerParams(collective_id=0, has_side_effects=True, vmem_limit_bytes=VLIM),
        name="panel_kernel",
    )(features)
    out_l, out_t = pl.pallas_call(
        update_kernel,
        out_shape=(jax.ShapeDtypeStruct((384, 256), F32), jax.ShapeDtypeStruct((2304, 128), F32)),
        in_specs=[vm] * 6,
        out_specs=(vm, pl.BlockSpec(memory_space=pl.ANY)),
        scratch_shapes=[pltpu.VMEM((384, F), BF), pltpu.VMEM((384, 128), F32), pltpu.VMEM((384, 256), F32),
                        pltpu.VMEM((768, F), BF), pltpu.VMEM((768, 128), F32), pltpu.VMEM((1, 768), F32),
                        pltpu.VMEM((768, 256), F32), pltpu.VMEM((2304, 128), F32), dma((3,))],
        compiler_params=pltpu.CompilerParams(vmem_limit_bytes=VLIM),
        name="update_kernel",
    )(*parts)
    return out_l.reshape(3, 1, 128, 256), out_t.reshape(3, 1, 128, 6, 1, 128)


def solution(mesh):
    return jax.shard_map(
        local,
        mesh=mesh,
        in_specs=(P(None, "row", "col", None),),
        out_specs=(P(None, "row", None, None), P(None, "row", None, None, "col", None)),
        check_vma=False,
    )
```

```python
import functools
import math

import jax
import jax.numpy as jnp
from jax import lax
from jax.experimental import pallas as pl
from jax.experimental.pallas import tpu as pltpu
from jax.sharding import PartitionSpec as P

MESH = pl.DeviceIdType.MESH

F = 512
F32 = jnp.float32
BF = jnp.bfloat16
IPI = 1.0 / math.pi
POLY = (1.5707963050, -0.2145988016, 0.0889789874, -0.0501743046,
        0.0308918810, -0.0170881256, 0.0066700901, -0.0012624911)
NT = (((1,), (1,)), ((), ()))
NN = (((1,), (0,)), ((), ()))
TN = (((0,), (0,)), ((), ()))


def dot(a, b, dims):
    return lax.dot_general(a, b, dims, preferred_element_type=F32)


def split(a):
    hi = a.astype(BF)
    return hi, (a - hi.astype(F32)).astype(BF)


def dot3(a, b, dims):
    return dot(a[0], b[0], dims) + (dot(a[0], b[1], dims) + dot(a[1], b[0], dims))


def half_angle(ax):
    y = jnp.maximum(1.0 - ax, 1e-30)
    s = y * lax.rsqrt(y)
    z = 1.0 + ax
    root = (s * IPI) * (z * lax.rsqrt(z))
    p = POLY[7] * IPI
    for c in POLY[6::-1]:
        p = p * ax + c * IPI
    return root, s * p


def ntk(gram, ur, uc, scale):
    t = gram * (ur * uc)
    root, w = half_angle(jnp.abs(t))
    h = jnp.where(t < 0.0, w, 1.0 - w)
    th = t * h
    jf = root + th
    theta = th + jf
    root2, w2 = half_angle(jnp.minimum(jf, 1.0))
    h2 = 1.0 - w2
    return (root2 + h2 * (theta + jf)) * scale


def squares(x):
    x = x.astype(F32)
    return split(x * x)


def col_form(sq):
    ones = jnp.ones((128, F), BF)
    return (dot(sq[0], ones, NT) + dot(sq[1], ones, NT)) * (1.0 / F) + 1e-6


def row_form(sq):
    ones = jnp.ones((8, F), BF)
    return (dot(ones, sq[0], NT) + dot(ones, sq[1], NT))[0:1] * (1.0 / F) + 1e-6


VLIM = 24 * 1024 * 1024


def at(ref, i):
    return ref[i * 128:(i + 1) * 128]


def tile(xa, qa, xb, qb, same):
    gram = dot(xa, xb, NT) * (1.0 / F)
    k = ntk(gram, lax.rsqrt(qa), lax.rsqrt(qb), jnp.sqrt(qa) * jnp.sqrt(qb))
    if same is False:
        return k
    ii = lax.broadcasted_iota(jnp.int32, (128, 128), 0)
    jj = lax.broadcasted_iota(jnp.int32, (128, 128), 1)
    eq = ii == jj if same is True else (ii == jj) & same
    return jnp.where(eq, gram + 2.0 * qa + 1.0, k)


NZ = 16
PANEL0 = 3
RING2, ROOT, RING4 = 9, 12, 18
LOOP = PANEL0 + NZ


def panel_kernel(B, x_ref, C, R, xp, qpr, w_hi, w_lo, Q, qpc, M,
                 lsem, zrecv, zsend, crecv, csend, cdir, csib, qrecv, qplane, qz, qsib):
    r = lax.axis_index("row")
    z = lax.axis_index("col")
    core = r % 2
    y = (r // 2) % 4
    x = r // 8
    N = 256
    is_root = (x == 0) & (y == 0)

    def rid(xx, yy, cc):
        return (((xx + 4) % 4) * 4 + ((yy + 4) % 4)) * 2 + cc

    own = pltpu.make_async_copy(x_ref.at[:, 0], R.at[z], lsem)
    own.start()
    sibling = (r + 1 - 2 * core, z)
    others = [((r + k) % 32, z) for k in range(2, 32, 2)] + [sibling]
    to_root = (2 * z + r // NZ, r % NZ)
    cb, co = core, r // 2
    from_z = (z + NZ * core, r // 2)
    alone = (to_root[0] == r) & (to_root[1] == z)

    plane = [(rid(x + k // 4, y + k % 4, core), z) for k in (10, 6, 14, 9, 11, 2, 8, 5, 7, 13, 15, 1, 3, 4, 12)]
    bar = pltpu.get_barrier_semaphore()

    def hello(p):
        pl.semaphore_signal(bar, inc=1, device_id=p, device_id_type=MESH)

    for p in [(r, (z + k) % NZ) for k in range(1, NZ)] + others:
        hello(p)

    @pl.when(alone)
    def _():
        pl.semaphore_wait(bar, NZ - 1 + len(others))

    @pl.when(jnp.logical_not(alone))
    def _():
        hello(to_root)
        hello(from_z)
        pl.semaphore_wait(bar, NZ - 1 + len(others) + 2)

    own.wait()

    def remote(src, dst, ssem, rsem, to):
        return pltpu.make_async_remote_copy(src_ref=src, dst_ref=dst, send_sem=ssem, recv_sem=rsem,
                                            device_id=to, device_id_type=MESH)

    mine = Q.at[core, z]

    @pl.when(is_root)
    def _():
        for k in range(15):
            remote(R.at[z, 0], mine, qplane.at[k], qrecv.at[core, z], plane[k]).start()
        pltpu.make_async_copy(R.at[z, 0], mine, qrecv.at[core, z]).start()

    @pl.when(alone)
    def _():
        pltpu.make_async_copy(R.at[z], C.at[r // NZ, z], crecv.at[r // NZ, z]).start()

    @pl.when(jnp.logical_not(alone))
    def _():
        remote(R.at[z], C.at[r // NZ, z], cdir, crecv.at[r // NZ, z], to_root).start()

    def zcopy(o, d, hops):
        return remote(R.at[o], R.at[o], zsend.at[(0 if d > 0 else 2) + hops - 1], zrecv.at[o],
                      (r, (z + d * hops + NZ) % NZ))

    def qwait(t, o):
        pltpu.make_async_copy(Q.at[t, o], Q.at[t, o], qrecv.at[t, o]).wait()

    def to_sibling(o):
        remote(Q.at[core, o], Q.at[core, o], qsib, qrecv.at[core, o], sibling).start()

    qwait(core, z)
    for k in (8, 7, 9, 6, 10, 5, 11, 4, 12, 3, 13, 2, 14, 1, 15):
        remote(mine, mine, qz.at[k - 1], qrecv.at[core, z], (r, (z + k) % NZ)).start()
    to_sibling(z)
    for hops in (2, 1):
        zcopy(z, 1, hops).start()
        zcopy(z, -1, hops).start()

    def seq(i):
        d = (i + 1) // 2
        return lax.rem(jnp.where(i % 2 == 1, z - d, z + d) + NZ, NZ)

    def panel_step(tau):
        i = tau - PANEL0

        @pl.when((i >= 1) & (i < NZ))
        def _():
            o = seq(i)
            qwait(core, o)
            to_sibling(o)

    def arrived(o):
        pltpu.make_async_copy(R.at[o], R.at[o], zrecv.at[o]).wait()

    def along_z(d):
        up, down = (z - d + NZ) % NZ, (z + d) % NZ
        arrived(up)
        if d < 8:
            zcopy(up, 1, 2).start()
            zcopy(up, 1, 1).start()
            arrived(down)
            if d < 6:
                zcopy(down, -1, 2).start()
            zcopy(down, -1, 1).start()
        arrived((z - d + 1 + NZ) % NZ)
        arrived((z + d - 1) % NZ)

    blk = C.at[cb, co]

    def cwait(b, o):
        pltpu.make_async_copy(C.at[b, o], C.at[b, o], crecv.at[b, o]).wait()

    def pass_on(k, carry):
        o = (co + k) % NZ
        cwait(cb, o)
        remote(C.at[cb, o], C.at[cb, o], csib, crecv.at[cb, o], sibling).start()
        return carry

    def step(tau, carry):
        panel_step(tau)

        @pl.when(tau == RING2)
        def _():
            along_z(2)

        @pl.when(tau == ROOT)
        def _():
            cwait(cb, co)
            for k in range(16):
                remote(blk, blk, csend.at[k], crecv.at[cb, co], others[k]).start()

        @pl.when(tau == RING4)
        def _():
            along_z(4)

        return carry

    lax.fori_loop(0, LOOP, step, 0)

    def from_sibling(o, carry):
        qwait(1 - core, o)
        return carry

    lax.fori_loop(0, NZ, from_sibling, 0)

    for t in range(2):
        v = Q[t].reshape(128, F)
        xp[t * 128:(t + 1) * 128] = v
        sq = squares(v)
        qpc[t * 128:(t + 1) * 128] = col_form(sq)
        qpr[:, t * 128:(t + 1) * 128] = row_form(sq)

    for i in range(2):
        for t in range(2):
            M[i * 128:(i + 1) * 128, t * 128:(t + 1) * 128] = tile(
                at(xp, i), at(qpc, i), at(xp, t), qpr[:, t * 128:(t + 1) * 128], i == t)
    ri = lax.broadcasted_iota(jnp.int32, (N, N), 0)
    ci = lax.broadcasted_iota(jnp.int32, (N, N), 1)
    M[:, N:2 * N] = jnp.where(ri == ci, 1.0, 0.0)

    def after_block(n):
        if n == 2:
            along_z(6)
        if n == 4:
            lax.fori_loop(1, NZ, pass_on, 0)
        if n == 6:
            along_z(8)

    sub = lax.broadcasted_iota(jnp.int32, (8, 128), 0)
    G = B // 8

    def wide(v):
        return jnp.broadcast_to(v, (8, 128))

    for n in range(N // B):
        lo = n * B
        hi = lo + B
        D = M[lo:hi, lo // 128 * 128:lo // 128 * 128 + 128]
        o = lo % 128
        col = [[wide(D[8 * g:8 * g + 8, o + k:o + k + 1]) if g >= k // 8 else None for g in range(G)]
               for k in range(B)]
        lanes = list(range(hi // 128, 2)) + list(range(2, 3 + (hi - 1) // 128))
        S = [[M[lo + 8 * g:lo + 8 * g + 8, 128 * v:128 * v + 128] for v in lanes] for g in range(G)]
        for k in range(B):
            gk = k // 8
            rs = wide(lax.rsqrt(col[k][gk])[k % 8:k % 8 + 1])
            c = [col[k][g] * rs if g >= gk else None for g in range(G)]
            for m in range(k + 1, B):
                f = wide(c[m // 8][m % 8:m % 8 + 1])
                for g in range(m // 8, G):
                    col[m][g] = col[m][g] - c[g] * f
            below = jnp.where(sub > k % 8, c[gk], 0.0)
            for v in range(len(lanes)):
                row = wide(S[gk][v][k % 8:k % 8 + 1]) * rs
                S[gk][v] = jnp.where(sub == k % 8, row, S[gk][v] - below * row)
                for g in range(gk + 1, G):
                    S[g][v] = S[g][v] - c[g] * row
        Y = [jnp.concatenate([S[g][v] for g in range(G)], axis=0) for v in range(len(lanes))]
        for v in range(len(lanes)):
            M[lo:hi, 128 * lanes[v]:128 * lanes[v] + 128] = Y[v]
        if hi < N:
            ys = [split(y) for y in Y]
            U = split(M[lo:hi, hi:N])
            for v in range(len(lanes)):
                cs = slice(128 * lanes[v], 128 * lanes[v] + 128)
                M[hi:, cs] = M[hi:, cs] - dot3(U, ys[v], TN)
        after_block(n)
    wf = split(M[:, N:])
    w_hi[...] = wf[0]
    w_lo[...] = wf[1]

    def sent(ref, sem):
        pltpu.make_async_copy(ref, ref, sem).wait()

    @pl.when(is_root)
    def _():
        for k in range(15):
            sent(mine, qplane.at[k])

    for k in range(15):
        sent(mine, qz.at[k])
    sent(Q.at[0], qsib)

    @pl.when(jnp.logical_not(alone))
    def _():
        sent(R.at[0], cdir)

    for k, n in ((0, 4), (1, 4), (2, 4), (3, 3)):
        sent(R.at[pl.ds(0, n)], zsend.at[k])
    for k in range(16):
        sent(blk, csend.at[k])
    sent(C.at[cb, pl.ds(0, NZ - 1)], csib)

    def rest(o, carry):
        cwait(1 - cb, o)
        return carry

    lax.fori_loop(0, NZ, rest, 0)


def update_kernel(C, R, xp, qpr, w_hi, w_lo, out_l, out_t, xr, qr, kr, xc, qc, qcr, kc, oslot, osem):
    r = lax.axis_index("row")
    z = lax.axis_index("col")
    w = (w_hi[...], w_lo[...])
    for a in range(3):
        v = R[:, a].reshape(128, F)
        xr[a * 128:(a + 1) * 128] = v
        qr[a * 128:(a + 1) * 128] = col_form(squares(v))
        for t in range(2):
            kr[a * 128:(a + 1) * 128, t * 128:(t + 1) * 128] = tile(
                at(xr, a), at(qr, a), at(xp, t), qpr[:, t * 128:(t + 1) * 128], (r == t) if a == 0 else False)
    lr = dot3(split(kr[...]), w, NT)
    out_l[...] = lr
    for a in range(3):
        for b in range(2):
            t = 2 * a + b
            v = C[b, :, a].reshape(128, F)
            xc[t * 128:(t + 1) * 128] = v
            sq = squares(v)
            qc[t * 128:(t + 1) * 128] = col_form(sq)
            qcr[:, t * 128:(t + 1) * 128] = row_form(sq)
    for i in range(6):
        for t in range(2):
            kc[i * 128:(i + 1) * 128, t * 128:(t + 1) * 128] = tile(
                at(xc, i), at(qc, i), at(xp, t), qpr[:, t * 128:(t + 1) * 128],
                (z == t) if i == 0 else False)
    lc = split(dot3(split(kc[...]), w, NT))
    lr = split(lr)
    copies = []
    for a in range(3):
        rows = slice(a * 128, (a + 1) * 128)
        for t in range(6):
            cols = slice(t * 128, (t + 1) * 128)
            k = tile(at(xr, a), at(qr, a), at(xc, t), qcr[:, cols],
                     (r == z + NZ * (t % 2)) if t // 2 == a else False)
            k = k - dot3(tuple(v[rows] for v in lr), tuple(v[cols] for v in lc), NT)
            oslot[pl.ds(a * 768 + t, 128, stride=6), :] = k
        c = pltpu.make_async_copy(oslot.at[pl.ds(a * 768, 768)], out_t.at[pl.ds(a * 768, 768)], osem.at[a])
        c.start()
        copies.append(c)
    for c in copies:
        c.wait()


def local(features):
    dma = pltpu.SemaphoreType.DMA
    vm = pl.BlockSpec(memory_space=pltpu.VMEM)
    parts = pl.pallas_call(
        functools.partial(panel_kernel, 32),
        out_shape=(jax.ShapeDtypeStruct((2, NZ, 3, 8, F), BF), jax.ShapeDtypeStruct((NZ, 3, 8, F), BF),
                   jax.ShapeDtypeStruct((256, F), BF), jax.ShapeDtypeStruct((1, 256), F32),
                   jax.ShapeDtypeStruct((256, 256), BF), jax.ShapeDtypeStruct((256, 256), BF)),
        in_specs=[pl.BlockSpec(memory_space=pl.ANY)],
        out_specs=(vm,) * 6,
        scratch_shapes=[pltpu.VMEM((2, NZ, 8, F), BF),
                        pltpu.VMEM((256, 128), F32), pltpu.VMEM((256, 512), F32),
                        dma, dma((NZ,)), dma((4,)), dma((2, NZ)), dma((16,)), dma, dma,
                        dma((2, NZ)), dma((15,)), dma((15,)), dma],
        compiler_params=pltpu.CompilerParams(collective_id=0, has_side_effects=True, vmem_limit_bytes=VLIM),
        name="panel_kernel",
    )(features)
    out_l, out_t = pl.pallas_call(
        update_kernel,
        out_shape=(jax.ShapeDtypeStruct((384, 256), F32), jax.ShapeDtypeStruct((2304, 128), F32)),
        in_specs=[vm] * 6,
        out_specs=(vm, pl.BlockSpec(memory_space=pl.ANY)),
        scratch_shapes=[pltpu.VMEM((384, F), BF), pltpu.VMEM((384, 128), F32), pltpu.VMEM((384, 256), F32),
                        pltpu.VMEM((768, F), BF), pltpu.VMEM((768, 128), F32), pltpu.VMEM((1, 768), F32),
                        pltpu.VMEM((768, 256), F32), pltpu.VMEM((2304, 128), F32), dma((3,))],
        compiler_params=pltpu.CompilerParams(vmem_limit_bytes=VLIM),
        name="update_kernel",
    )(*parts)
    return out_l.reshape(3, 1, 128, 256), out_t.reshape(3, 1, 128, 6, 1, 128)


def solution(mesh):
    return jax.shard_map(
        local,
        mesh=mesh,
        in_specs=(P(None, "row", "col", None),),
        out_specs=(P(None, "row", None, None), P(None, "row", None, None, "col", None)),
        check_vma=False,
    )
```
